128 devices in a mesh: wall: 16 (over y, z), span: 4 (over x), stream: 2 (over core).
Axes of the slice: x: 4, y: 4, z: 4, core: 2. Of those that a mesh axis runs over, the one named last changes fastest.
Arguments:
- conserved: float32 [5, 32, 1536, 512], P(None, 'stream', 'wall', 'span'), may hold values from -6 to 6
- wall_metric: float32 [32, 1536, 512], P('stream', 'wall', 'span'), may hold values from 0.5 to 4
- span_metric: float32 [32, 1536, 512], P('stream', 'wall', 'span'), may hold values from 0.5 to 4
Outputs:
- wall_slope: float32 [5, 32, 1536, 512], P(None, 'stream', 'wall', 'span')
- span_slope: float32 [5, 32, 1536, 512], P(None, 'stream', 'wall', 'span')
The draws below stay inside these ranges and needn't reach their ends.
All inputs are finite; a program needn't handle non-finite values.
Results may differ from the reference program's by a relative error of at most 0.0003.
Values sent between devices are 32-bit elements; how exact they have to be, the bound alone decides.
No kernel may reach another device: no remote copies, remote signals or barrier semaphores. Data moves between devices by JAX's collectives and lax.ppermute only.
A program may use at most 128 MiB of HBM per device.

```python
import math
import jax
import jax.numpy as jnp
import numpy as np
from jax import lax

FIELDS = 5
PLANES = 32
NW = 1536
NS = 512


def block_scale(stream_key, shape, pieces, least, largest):
    def one(axis_at, shards_of):
        heights = jax.random.uniform(jax.random.fold_in(jax.random.fold_in(stream_key, 6), axis_at), (shards_of,), jnp.float32, least / len(pieces), largest / len(pieces))
        return jnp.repeat(jnp.exp(heights), shape[axis_at] // shards_of).reshape((-1,) + (1,) * (len(shape) - axis_at - 1))

    gain = one(*pieces[0])
    for cut in pieces[1:]:
        gain = gain * one(*cut)
    return gain


def gaussian(own_key, shape, spread, limit, pieces=(), kind=jnp.bfloat16):
    level = block_scale(own_key, shape, pieces, -0.22, 0.18) if pieces else 1.0
    values = jax.random.normal(own_key, shape, jnp.float32) * spread * level
    return jnp.minimum(jnp.maximum(values, -limit), limit).astype(kind)


def setup_inputs(seed: int = 0) -> dict:
    streams_of = jax.random.split(jax.random.key(seed), 4)
    conserved = gaussian(streams_of[0], (FIELDS, PLANES, NW, NS), 1.0, 6.0, ((1, 2), (2, 16), (3, 4)), jnp.float32)
    wall_metric = jnp.clip(jnp.exp(math.log(4.0) - 2.0794415 * jax.random.uniform(streams_of[1], (PLANES, NW, NS), jnp.float32) ** block_scale(streams_of[1], (PLANES, NW, NS), ((0, 2), (1, 16), (2, 4)), -0.2, 0.2)), 0.5, 4.0)
    span_metric = jnp.clip(jnp.exp(math.log(4.0) - 2.0794415 * jax.random.uniform(streams_of[2], (PLANES, NW, NS), jnp.float32) ** block_scale(streams_of[2], (PLANES, NW, NS), ((0, 2), (1, 16), (2, 4)), -0.2, 0.2)), 0.5, 4.0)
    return dict(conserved=conserved, wall_metric=wall_metric, span_metric=span_metric)


band_alpha = 0.4995


def line_coefficients(length_all):
    lower_band = np.full(length_all, band_alpha)
    lower_band[1] = 0.25
    lower_band[length_all - 2] = 0.25
    lower_band[0] = 0.0
    lower_band[length_all - 1] = 0.0
    scales = np.zeros(length_all)
    pivots = np.zeros(length_all)
    previous = 0.0
    for row_idx in range(length_all):
        scales[row_idx] = 1.0 / (1.0 - lower_band[row_idx] * previous)
        pivots[row_idx] = lower_band[row_idx] * scales[row_idx]
        previous = pivots[row_idx]
    near_coef = (band_alpha + 2.0) / 3.0
    far_coef = (4.0 * band_alpha - 1.0) / 12.0
    weights = np.zeros((5, length_all))
    weights[:, :] = np.array([-far_coef, -near_coef, 0.0, near_coef, far_coef])[:, None]
    weights[:, 1] = [0.0, -0.75, 0.0, 0.75, 0.0]
    weights[:, length_all - 2] = [0.0, -0.75, 0.0, 0.75, 0.0]
    weights[:, 0] = [0.0, 0.0, -1.5, 2.0, -0.5]
    weights[:, length_all - 1] = [0.5, -2.0, 1.5, 0.0, 0.0]
    return lower_band, scales, pivots, weights


def line_slope(conserved, axis_pos):
    length_all = conserved.shape[axis_pos]
    lower_band, scales, pivots, weights = line_coefficients(length_all)
    line_data = jnp.moveaxis(conserved, axis_pos, 0)
    padded = jnp.pad(line_data, ((2, 2), (0, 0), (0, 0), (0, 0)))
    right_side = 0.0
    for offset in range(5):
        coefficient = jnp.asarray(weights[offset], jnp.float32)[:, None, None, None]
        right_side = right_side + coefficient * padded[offset:offset + length_all]
    band_low = jnp.asarray(lower_band, jnp.float32)
    band_scale = jnp.asarray(scales, jnp.float32)
    band_pivot = jnp.asarray(pivots, jnp.float32)

    def forward(running, row_item):
        row_value, lower_coef, scale_coef = row_item
        updated = (row_value - lower_coef * running) * scale_coef
        return updated, updated

    def backward(running, row_item):
        row_value, pivot_coef = row_item
        updated = row_value - pivot_coef * running
        return updated, updated

    start_row = jnp.zeros(line_data.shape[1:], jnp.float32)
    _, reduced = lax.scan(forward, start_row, (right_side, band_low, band_scale))
    _, slopes = lax.scan(backward, start_row, (reduced, band_pivot), reverse=True)
    return jnp.moveaxis(slopes, 0, axis_pos)


def reference(conserved, wall_metric, span_metric):
    wall_part = line_slope(conserved, 2)
    span_part = line_slope(conserved, 3)
    return wall_metric[None] * wall_part, span_metric[None] * span_part
```

```python
import functools

import jax
import jax.numpy as jnp
import numpy as np
from jax import lax
from jax.experimental import pallas as pl
from jax.experimental.pallas import tpu as pltpu
from jax.sharding import PartitionSpec as P

F32 = jnp.float32
BF16 = jnp.bfloat16
band_alpha = 0.4995
LANES = 128
VMEM_LIMIT = 16 * 2**20


def line_coefficients(length_all):
    lower_band = np.full(length_all, band_alpha)
    lower_band[1] = 0.25
    lower_band[length_all - 2] = 0.25
    lower_band[0] = 0.0
    lower_band[length_all - 1] = 0.0
    scales = np.zeros(length_all)
    pivots = np.zeros(length_all)
    previous = 0.0
    for row_idx in range(length_all):
        scales[row_idx] = 1.0 / (1.0 - lower_band[row_idx] * previous)
        pivots[row_idx] = lower_band[row_idx] * scales[row_idx]
        previous = pivots[row_idx]
    near_coef = (band_alpha + 2.0) / 3.0
    far_coef = (4.0 * band_alpha - 1.0) / 12.0
    weights = np.zeros((5, length_all))
    weights[:, :] = np.array([-far_coef, -near_coef, 0.0, near_coef, far_coef])[:, None]
    weights[:, 1] = [0.0, -0.75, 0.0, 0.75, 0.0]
    weights[:, length_all - 2] = [0.0, -0.75, 0.0, 0.75, 0.0]
    weights[:, 0] = [0.0, 0.0, -1.5, 2.0, -0.5]
    weights[:, length_all - 1] = [0.5, -2.0, 1.5, 0.0, 0.0]
    return (lower_band, scales, pivots, weights)


@functools.lru_cache(maxsize=None)
def line_tables(length_all, pieces):
    block = length_all // pieces
    lower_band, scales, pivots, weights = line_coefficients(length_all)

    def solve(rows):
        out = np.zeros_like(rows)
        running = np.zeros(rows.shape[1])
        for i in range(length_all):
            running = (rows[i] - lower_band[i] * running) * scales[i]
            out[i] = running
        running = np.zeros(rows.shape[1])
        for i in range(length_all - 1, -1, -1):
            running = out[i] - pivots[i] * running
            out[i] = running
        return out

    stencil = np.zeros((length_all, length_all))
    for k in range(5):
        for g in range(length_all):
            if 0 <= g + k - 2 < length_all:
                stencil[g, g + k - 2] = weights[k, g]
    whole = solve(stencil)
    unit = np.zeros((length_all, 2 * pieces))
    for k in range(pieces):
        unit[k * block, k] = 1.0
        unit[k * block + block - 1, pieces + k] = 1.0
    inverse = solve(unit)
    t = {
        "diag": np.zeros((pieces, block, block)),
        "enter": np.zeros((pieces, block)),
        "leave": np.zeros((pieces, block)),
        "right": np.zeros((pieces, block)),
        "left": np.zeros((pieces, block)),
        "first": np.zeros(pieces),
        "last": np.zeros(pieces),
        "pass_right": np.ones(pieces),
        "pass_left": np.ones(pieces),
    }
    for k in range(pieces):
        lo, hi = k * block, k * block + block
        t["diag"][k] = whole[lo:hi, lo:hi]
        t["enter"][k] = inverse[lo:hi, k] / inverse[lo, k]
        t["leave"][k] = inverse[lo:hi, pieces + k] / inverse[hi - 1, pieces + k]
        if k < pieces - 1:
            t["pass_right"][k] = inverse[hi, k] / inverse[lo, k]
        if k > 0:
            t["pass_left"][k] = inverse[lo - 1, pieces + k] / inverse[hi - 1, pieces + k]
    for k in range(pieces):
        lo, hi = k * block, k * block + block
        if k < pieces - 1:
            t["right"][k] = whole[hi + 1, lo:hi] / t["enter"][k + 1][1]
        if k > 0:
            t["left"][k] = whole[lo - 2, lo:hi] / t["leave"][k - 1][block - 2]
    for k in range(pieces):
        lo, hi = k * block, k * block + block
        if k > 0:
            t["first"][k] = whole[lo, lo - 1] - t["right"][k - 1][block - 1]
        if k < pieces - 1:
            t["last"][k] = whole[hi - 1, hi] - t["left"][k + 1][0]
    return t


def doubling_coefficients(t, pieces):
    rounds = pieces.bit_length() - 1
    right, left = t["pass_right"], t["pass_left"]
    coef = np.zeros((pieces, rounds, 8))
    for r in range(rounds):
        half = 1 << r
        for k in range(pieces):
            base = k // half * half
            inside = slice(base, base + half)
            if (k // half) % 2:
                other = slice(base - half, base)
                coef[k, r, :6] = [np.prod(right[base:k]), 0.0, 1.0, np.prod(right[inside]), np.prod(left[other]), 1.0]
            else:
                other = slice(base + half, base + 2 * half)
                coef[k, r, :6] = [0.0, np.prod(left[k + 1 : base + half]), np.prod(right[other]), 1.0, 1.0, np.prod(left[inside])]
    for k in range(pieces):
        if k > 0:
            coef[k, halo_round(k - 1), 6] = t["first"][k]
        if k < pieces - 1:
            coef[k, halo_round(k), 7] = t["last"][k]
    pick = np.array([[float(k >= pieces // 2), float(k < pieces // 2)] for k in range(pieces)])
    return np.concatenate([coef.reshape(pieces, -1), pick], axis=1)


def halo_round(k):
    if k % 2 == 0:
        return 0
    if k % 4 == 1:
        return 1
    return 2 if k % 8 == 3 else 3


def split_table(x):
    x = np.asarray(x, np.float32)
    high = x.astype(BF16)
    rest = x - high.astype(np.float32)
    mid = rest.astype(BF16)
    low = (rest - mid.astype(np.float32)).astype(BF16)
    return high, mid, low


def split_parts(x):
    high = x.astype(BF16)
    rest = x - high.astype(F32)
    mid = rest.astype(BF16)
    low = (rest - mid.astype(F32)).astype(BF16)
    return high, mid, low


def dot(a, b, dims):
    return lax.dot_general(a, b, (dims, ((), ())), preferred_element_type=F32)


COEF_ROWS = 40
STEP = 8


def table_loads(sources, targets, sems, wall_count):
    for j, (source, target) in enumerate(zip(sources, targets)):
        at = lax.axis_index("wall") if j < wall_count else lax.axis_index("span")
        yield pltpu.make_async_copy(source.at[at], target, sems.at[j])


def wall_moment_kernel(x_hbm, *refs):
    sources, targets = refs[:7], refs[7:14]
    x_ref, pay_ref, other_ref, x_sems, t_sems = refs[14:]
    fields, planes, rows, _ = x_ref.shape
    per = planes // STEP

    def x_copy(i):
        piece = (i // per, pl.ds(i % per * STEP, STEP))
        return pltpu.make_async_copy(x_hbm.at[piece], x_ref.at[piece], x_sems.at[i])

    loads = list(table_loads(sources, targets, t_sems, 3))
    loads[0].start()
    for i in range(fields * per):
        x_copy(i).start()
    for load in loads[1:]:
        load.start()
    loads[0].wait()
    even = lax.axis_index("wall") % 2 == 0
    table = targets[0][...]
    right, left = table[:, 0:1], table[:, 1:2]

    def chunk(i, carry):
        x_copy(i).wait()
        f, at = i // per, pl.ds(i % per * STEP, STEP)
        x = x_ref[f, at]
        pay_ref[0, f, at] = jnp.sum(x * right[None], axis=1)
        pay_ref[1, f, at] = jnp.sum(x * left[None], axis=1)
        first, last = x[:, 0, :], x[:, rows - 1, :]
        pay_ref[2, f, at] = jnp.where(even, last, first)
        other_ref[f, at] = jnp.where(even, first, last)
        return carry

    lax.fori_loop(0, fields * per, chunk, 0)
    for load in loads[1:]:
        load.wait()


def wall_merge_kernel(last, first_round, sent_ref, got_ref, extra_ref, *refs):
    if first_round:
        coef_ref, pay_ref, state_ref = refs
    else:
        old_ref, coef_ref, pay_ref, state_ref = refs
    coef = coef_ref[...]

    def c(j):
        return coef[j : j + 1, 0:1]

    base = 0 if first_round else (16 if last else 8)
    got_r, got_l, halo = got_ref[0], got_ref[1], got_ref[2]
    for j, value in enumerate((c(base) * got_r, c(base + 1) * got_l, c(base + 6) * halo, c(base + 7) * halo)):
        state_ref[j] = value if first_round else old_ref[j] + value
    own_r = c(base + 2) * sent_ref[0] + c(base + 3) * got_r
    own_l = c(base + 4) * sent_ref[1] + c(base + 5) * got_l
    if last:
        pay_ref[0] = c(32) * own_l + c(33) * own_r
        pay_ref[1] = extra_ref[...]
    else:
        pay_ref[0] = own_r
        pay_ref[1] = own_l
        pay_ref[2] = extra_ref[...]


def wall_local_kernel(x_ref, table_ref, out_ref):
    fields, planes, block, lanes = x_ref.shape
    per = planes // STEP
    table = table_ref[...]
    pad = table.shape[1] - block
    d_high, d_mid, d_low = table[:block], table[block : 2 * block], table[2 * block :]
    lhs = jnp.concatenate([jnp.concatenate([d_high, d_high], axis=1), jnp.concatenate([d_mid, d_mid], axis=1)], axis=0)
    lhs2 = jnp.concatenate([d_high, d_low], axis=1)

    def stacked(a, b):
        return jnp.concatenate([a, a[:pad], b, b[:pad]], axis=0)

    def chunk(i, carry):
        f, q = i // per, i % per * STEP
        flat = jnp.concatenate([x_ref[f, q + j] for j in range(STEP)], axis=1)
        high, mid, low = split_parts(flat)
        main = dot(lhs, stacked(high, mid), ((1,), (0,)))
        rest = dot(lhs2, stacked(low, high), ((1,), (0,)))
        total = main[:block] + (main[block:] + rest)
        for j in range(STEP):
            out_ref[f, q + j] = total[:, j * lanes : (j + 1) * lanes]
        return carry

    lax.fori_loop(0, fields * per, chunk, 0)


def store_loop(count, per, out_hbm, buffer, sems, compute):
    def copy(i, slot):
        return pltpu.make_async_copy(buffer.at[slot], out_hbm.at[i // per, pl.ds(i % per * STEP, STEP)], sems.at[slot])

    def chunk(i, carry):
        slot = i % 2

        @pl.when(i >= 2)
        def _():
            copy(i - 2, slot).wait()

        compute(i // per, pl.ds(i % per * STEP, STEP), i, buffer.at[slot])
        copy(i, slot).start()
        return carry

    lax.fori_loop(0, count, chunk, 0)
    copy(count - 2, count % 2).wait()
    copy(count - 1, (count - 1) % 2).wait()


def wall_final_kernel(local_ref, metric_ref, old_ref, got_ref, coef_ref, table_ref, out_hbm, buffer, sems):
    fields, planes, block, lanes = local_ref.shape
    per = planes // STEP
    coef = coef_ref[...]
    table = table_ref[...]
    enter, leave = table[:, 2:3], table[:, 3:4]
    top = lax.broadcasted_iota(jnp.int32, (1, 8, 1), 1) == 0
    bottom = lax.broadcasted_iota(jnp.int32, (1, 8, 1), 1) == 7

    def c(j):
        return coef[j : j + 1, 0:1]

    def compute(f, at, i, out):
        got, halo = got_ref[0, f, at], got_ref[1, f, at]
        m, n = old_ref[0, f, at] + c(24) * got, old_ref[1, f, at] + c(25) * got
        first, last = old_ref[2, f, at] + c(30) * halo, old_ref[3, f, at] + c(31) * halo
        for lo, hi in ((0, 8), (8, block - 8), (block - 8, block)):
            total = local_ref[f, at, lo:hi] + enter[None, lo:hi] * m[:, None, :] + leave[None, lo:hi] * n[:, None, :]
            if lo == 0:
                total = total + jnp.where(top, first[:, None, :], 0.0)
            if hi == block:
                total = total + jnp.where(bottom, last[:, None, :], 0.0)
            out[:, lo:hi] = metric_ref[at, lo:hi] * total

    store_loop(fields * per, per, out_hbm, buffer, sems, compute)


def span_moment_kernel(x_ref, table_ref, pay_ref, other_ref):
    fields, planes, rows, columns = x_ref.shape
    per = planes // STEP
    even = lax.axis_index("span") % 2 == 0
    table = table_ref[...]

    def chunk(i, carry):
        flat = x_ref[i // per, pl.ds(i % per * STEP, STEP)].reshape(STEP * rows, columns)
        high, mid, low = split_parts(flat)
        main = dot(table[:16], jnp.concatenate([high, mid], axis=1), ((1,), (1,)))
        rest = dot(table[16:], jnp.concatenate([low, high], axis=1), ((1,), (1,)))
        total = main[:8] + (main[8:] + rest[:8])
        first, last = total[2:3], total[3:4]
        at = pl.ds(pl.multiple_of(i * STEP * rows, 128), STEP * rows)
        pay_ref[0:2, at] = total[0:2]
        pay_ref[2:3, at] = jnp.where(even, last, first)
        other_ref[:, at] = jnp.where(even, first, last)
        return carry

    lax.fori_loop(0, fields * per, chunk, 0)


def span_merge_kernel(sent_ref, got_ref, other_ref, coef_ref, pay_ref, state_ref):
    coef = coef_ref[...]

    def c(j):
        return coef[j : j + 1, 0:1]

    got_r, got_l, halo = got_ref[0:1], got_ref[1:2], got_ref[2:3]
    for j, value in enumerate((c(0) * got_r, c(1) * got_l, c(6) * halo, c(7) * halo)):
        state_ref[j : j + 1] = value
    own_r = c(2) * sent_ref[0:1] + c(3) * got_r
    own_l = c(4) * sent_ref[1:2] + c(5) * got_l
    pay_ref[0:1] = c(16) * own_l + c(17) * own_r
    pay_ref[1:2] = other_ref[...]


def span_final_kernel(x_ref, metric_ref, old_ref, got_ref, coef_ref, table_ref, edge_ref, out_hbm, buffer, sems):
    fields, planes, rows, n = x_ref.shape
    per = planes // STEP
    coef = coef_ref[...]
    table = table_ref[...]
    d_high, d_low = table[:, :n], table[:, 2 * n :]
    weights = jnp.concatenate([table[:, : 2 * n], table[:, : 2 * n]], axis=0)
    weights2 = jnp.concatenate([d_high, d_low], axis=0)

    def c(j):
        return coef[j : j + 1, 0:1]

    def compute(f, at, i, out):
        flat = x_ref[f, at].reshape(STEP * rows, n)
        high, mid, low = split_parts(flat)
        main = dot(jnp.concatenate([high, mid], axis=1), weights, ((1,), (0,)))
        rest = dot(jnp.concatenate([low, high], axis=1), weights2, ((1,), (0,)))
        line = pl.ds(pl.multiple_of(i * STEP * rows, 128), STEP * rows)
        got, halo, old = got_ref[0:1, line], got_ref[1:2, line], old_ref[:, line]
        state = jnp.concatenate(
            [old[0:1] + c(8) * got, old[1:2] + c(9) * got, old[2:3] + c(14) * halo, old[3:4] + c(15) * halo]
            + [jnp.zeros((4, STEP * rows), F32)]
        )
        s_high = state.astype(BF16).astype(F32)
        s_rest = state - s_high
        s_mid = s_rest.astype(BF16).astype(F32)
        s_low = s_rest - s_mid
        parts = jnp.concatenate([s_high, s_high, s_mid, s_high, s_mid, s_low], axis=0).astype(BF16)
        edge = dot(parts, edge_ref[...], ((0,), (0,)))
        total = main[:, :n] + (main[:, n:] + (rest + edge))
        out[...] = metric_ref[at] * total.reshape(STEP, rows, n)

    store_loop(fields * per, per, out_hbm, buffer, sems, compute)


def per_device(conserved, wall_metric, span_metric):
    fields, planes, rows, columns = conserved.shape
    wall_pieces, span_pieces = lax.axis_size("wall"), lax.axis_size("span")
    wt = line_tables(rows * wall_pieces, wall_pieces)
    st = line_tables(columns * span_pieces, span_pieces)
    chunks = fields * planes // STEP
    lines = fields * planes * rows
    vmem = pl.BlockSpec(memory_space=pltpu.VMEM)
    hbm = pl.BlockSpec(memory_space=pltpu.HBM)

    def shape(*dims, dtype=F32):
        return jax.ShapeDtypeStruct(dims, dtype)

    def call(kernel, in_specs, out_specs, out_shape, micros, name, scratch=()):
        return pl.pallas_call(
            kernel,
            in_specs=in_specs,
            out_specs=out_specs,
            out_shape=out_shape,
            scratch_shapes=list(scratch),
            compiler_params=pltpu.CompilerParams(vmem_limit_bytes=VMEM_LIMIT),
            cost_estimate=pl.CostEstimate(flops=0, transcendentals=0, bytes_accessed=int(micros * 3.0e6)),
            name=name,
        )

    wall_rows = np.zeros((wall_pieces, rows, LANES), np.float32)
    for j, key in enumerate(("right", "left", "enter", "leave")):
        wall_rows[:, :, j] = wt[key]
    wall_diag = np.zeros((wall_pieces, 3 * rows, LANES), BF16)
    wall_diag[:, :, :rows] = np.concatenate(split_table(wt["diag"]), axis=1)
    span_diag = np.concatenate(split_table(np.swapaxes(st["diag"], 1, 2)), axis=2)
    pick = np.zeros((span_pieces, 4, columns))
    pick[:, 0], pick[:, 1] = st["right"], st["left"]
    pick[:, 2, 0] = 1.0
    pick[:, 3, columns - 1] = 1.0
    p_high, p_mid, p_low = split_table(pick)
    span_pick = np.zeros((span_pieces, 32, 2 * columns), BF16)
    span_pick[:, 0:4] = np.concatenate([p_high, p_high], axis=2)
    span_pick[:, 8:12] = np.concatenate([p_mid, p_mid], axis=2)
    span_pick[:, 16:20] = np.concatenate([p_high, p_low], axis=2)
    spread = np.zeros((span_pieces, 8, columns))
    spread[:, 0], spread[:, 1] = st["enter"], st["leave"]
    spread[:, 2, 0] = 1.0
    spread[:, 3, columns - 1] = 1.0
    e_high, e_mid, e_low = split_table(spread)
    span_edge = np.concatenate([e_high, e_mid, e_high, e_low, e_mid, e_high], axis=1)

    def spread_coefficients(t, pieces):
        c = doubling_coefficients(t, pieces)
        out = np.zeros((pieces, COEF_ROWS, LANES), np.float32)
        out[:, : c.shape[1]] = c[:, :, None]
        return out

    tables = [wall_rows, wall_diag, spread_coefficients(wt, wall_pieces)]
    tables += [span_diag, span_pick, span_edge, spread_coefficients(st, span_pieces)]
    tables = [pltpu.with_memory_space_constraint(jnp.asarray(t), pltpu.HBM) for t in tables]
    grid_values = pltpu.with_memory_space_constraint(conserved, pltpu.HBM)

    state = shape(4, fields, planes, columns)
    moment = shape(3, fields, planes, columns)
    out = call(
        wall_moment_kernel,
        [hbm] * 8,
        [vmem] * 10,
        [shape(*t.shape[1:], dtype=t.dtype) for t in tables]
        + [shape(*conserved.shape), moment, shape(fields, planes, columns)],
        2.5, "wall_moments",
        [pltpu.SemaphoreType.DMA((chunks,)), pltpu.SemaphoreType.DMA((len(tables),))],
    )(grid_values, *tables)
    w_rows, w_diag, w_coef, s_diag, s_pick, s_edge, s_coef, x, pay_w, other_w = out

    def swap(flip, pieces):
        return [(k, k ^ flip) for k in range(pieces)]

    got_w = lax.ppermute(pay_w, "wall", swap(1, wall_pieces))

    pay_s, other_s = call(
        span_moment_kernel, [vmem] * 2, [vmem] * 2, [shape(3, lines), shape(1, lines)], 3.4, "span_moments"
    )(x, s_pick)
    got_s = lax.ppermute(pay_s, "span", swap(1, span_pieces))

    pay_w, state_w = call(
        functools.partial(wall_merge_kernel, False, True), [vmem] * 4, [vmem] * 2, [moment, state], 0.2, "wall_merge_0"
    )(pay_w, got_w, other_w, w_coef)
    got_w = lax.ppermute(pay_w, "wall", swap(3, wall_pieces))
    halo = got_w[2]

    local_w = call(
        wall_local_kernel, [vmem] * 2, vmem, shape(*conserved.shape), 3.5, "wall_local"
    )(x, w_diag)

    pay_s, state_s = call(
        span_merge_kernel, [vmem] * 4, [vmem] * 2, [shape(2, lines), shape(4, lines)], 0.2, "span_merge"
    )(pay_s, got_s, other_s, s_coef)
    got_s = lax.ppermute(pay_s, "span", swap(3, span_pieces))

    pay_w, state_w = call(
        functools.partial(wall_merge_kernel, False, False), [vmem] * 5, [vmem] * 2, [moment, state], 0.2, "wall_merge_1"
    )(pay_w, got_w, halo, state_w, w_coef)
    got_w = lax.ppermute(pay_w, "wall", swap(4, wall_pieces))

    pay_w, state_w = call(
        functools.partial(wall_merge_kernel, True, False), [vmem] * 5, [vmem] * 2,
        [shape(2, fields, planes, columns), state], 0.2, "wall_merge_2",
    )(pay_w, got_w, halo, state_w, w_coef)
    got_w = lax.ppermute(pay_w, "wall", swap(12, wall_pieces))

    buffers = [pltpu.VMEM((2, STEP, rows, columns), F32), pltpu.SemaphoreType.DMA((2,))]
    span_slope = call(
        span_final_kernel, [vmem] * 7, hbm, shape(*conserved.shape), 6.0, "span_final", buffers
    )(x, span_metric, state_s, got_s, s_coef, s_diag, s_edge)
    wall_slope = call(
        wall_final_kernel, [vmem] * 6, hbm, shape(*conserved.shape), 4.0, "wall_final", buffers
    )(local_w, wall_metric, state_w, got_w, w_coef, w_rows)
    return (wall_slope, span_slope)


def solution(mesh):
    in_specs = (
        P(None, "stream", "wall", "span"),
        P("stream", "wall", "span"),
        P("stream", "wall", "span"),
    )
    out_specs = (P(None, "stream", "wall", "span"), P(None, "stream", "wall", "span"))
    return jax.shard_map(
        per_device, mesh=mesh, in_specs=in_specs, out_specs=out_specs, check_vma=False
    )
```

```python
import functools

import jax
import jax.numpy as jnp
import numpy as np
from jax import lax
from jax.experimental import pallas as pl
from jax.experimental.pallas import tpu as pltpu
from jax.sharding import PartitionSpec as P


F32 = jnp.float32
BF16 = jnp.bfloat16
band_alpha = 0.4995
LANES = 128
VMEM_LIMIT = 24 * 2**20


def line_coefficients(length_all):
    lower_band = np.full(length_all, band_alpha)
    lower_band[1] = 0.25
    lower_band[length_all - 2] = 0.25
    lower_band[0] = 0.0
    lower_band[length_all - 1] = 0.0
    scales = np.zeros(length_all)
    pivots = np.zeros(length_all)
    previous = 0.0
    for row_idx in range(length_all):
        scales[row_idx] = 1.0 / (1.0 - lower_band[row_idx] * previous)
        pivots[row_idx] = lower_band[row_idx] * scales[row_idx]
        previous = pivots[row_idx]
    near_coef = (band_alpha + 2.0) / 3.0
    far_coef = (4.0 * band_alpha - 1.0) / 12.0
    weights = np.zeros((5, length_all))
    weights[:, :] = np.array([-far_coef, -near_coef, 0.0, near_coef, far_coef])[:, None]
    weights[:, 1] = [0.0, -0.75, 0.0, 0.75, 0.0]
    weights[:, length_all - 2] = [0.0, -0.75, 0.0, 0.75, 0.0]
    weights[:, 0] = [0.0, 0.0, -1.5, 2.0, -0.5]
    weights[:, length_all - 1] = [0.5, -2.0, 1.5, 0.0, 0.0]
    return (lower_band, scales, pivots, weights)


@functools.lru_cache(maxsize=None)
def line_tables(length_all, pieces):
    block = length_all // pieces
    lower_band, scales, pivots, weights = line_coefficients(length_all)

    def solve(rows):
        out = np.zeros_like(rows)
        running = np.zeros(rows.shape[1])
        for i in range(length_all):
            running = (rows[i] - lower_band[i] * running) * scales[i]
            out[i] = running
        running = np.zeros(rows.shape[1])
        for i in range(length_all - 1, -1, -1):
            running = out[i] - pivots[i] * running
            out[i] = running
        return out

    stencil = np.zeros((length_all, length_all))
    for k in range(5):
        for g in range(length_all):
            if 0 <= g + k - 2 < length_all:
                stencil[g, g + k - 2] = weights[k, g]
    whole = solve(stencil)
    unit = np.zeros((length_all, 2 * pieces))
    for k in range(pieces):
        unit[k * block, k] = 1.0
        unit[k * block + block - 1, pieces + k] = 1.0
    inverse = solve(unit)
    t = {
        "diag": np.zeros((pieces, block, block)),
        "enter": np.zeros((pieces, block)),
        "leave": np.zeros((pieces, block)),
        "right": np.zeros((pieces, block)),
        "left": np.zeros((pieces, block)),
        "first": np.zeros(pieces),
        "last": np.zeros(pieces),
        "pass_right": np.ones(pieces),
        "pass_left": np.ones(pieces),
    }
    for k in range(pieces):
        lo, hi = k * block, k * block + block
        t["diag"][k] = whole[lo:hi, lo:hi]
        t["enter"][k] = inverse[lo:hi, k] / inverse[lo, k]
        t["leave"][k] = inverse[lo:hi, pieces + k] / inverse[hi - 1, pieces + k]
        if k < pieces - 1:
            t["pass_right"][k] = inverse[hi, k] / inverse[lo, k]
        if k > 0:
            t["pass_left"][k] = inverse[lo - 1, pieces + k] / inverse[hi - 1, pieces + k]
    for k in range(pieces):
        lo, hi = k * block, k * block + block
        if k < pieces - 1:
            t["right"][k] = whole[hi + 1, lo:hi] / t["enter"][k + 1][1]
        if k > 0:
            t["left"][k] = whole[lo - 2, lo:hi] / t["leave"][k - 1][block - 2]
    for k in range(pieces):
        lo, hi = k * block, k * block + block
        if k > 0:
            t["first"][k] = whole[lo, lo - 1] - t["right"][k - 1][block - 1]
        if k < pieces - 1:
            t["last"][k] = whole[hi - 1, hi] - t["left"][k + 1][0]
    return t


def doubling_coefficients(t, pieces):
    rounds = pieces.bit_length() - 1
    right, left = t["pass_right"], t["pass_left"]
    coef = np.zeros((pieces, rounds, 8))
    for r in range(rounds):
        half = 1 << r
        for k in range(pieces):
            base = k // half * half
            inside = slice(base, base + half)
            if (k // half) % 2:
                other = slice(base - half, base)
                coef[k, r, :6] = [np.prod(right[base:k]), 0.0, 1.0, np.prod(right[inside]), np.prod(left[other]), 1.0]
            else:
                other = slice(base + half, base + 2 * half)
                coef[k, r, :6] = [0.0, np.prod(left[k + 1 : base + half]), np.prod(right[other]), 1.0, 1.0, np.prod(left[inside])]
    for k in range(pieces):
        if k > 0:
            coef[k, halo_round(k - 1), 6] = t["first"][k]
        if k < pieces - 1:
            coef[k, halo_round(k), 7] = t["last"][k]
    pick = np.array([[float(k >= pieces // 2), float(k < pieces // 2)] for k in range(pieces)])
    return np.concatenate([coef.reshape(pieces, -1), pick], axis=1)


def halo_round(k):
    if k % 2 == 0:
        return 0
    if k % 4 == 1:
        return 1
    return 2 if k % 8 == 3 else 3


def split_table(x):
    x = np.asarray(x, np.float32)
    high = x.astype(BF16)
    rest = x - high.astype(np.float32)
    mid = rest.astype(BF16)
    low = (rest - mid.astype(np.float32)).astype(BF16)
    return high, mid, low


def split_parts(x):
    high = x.astype(BF16)
    rest = x - high.astype(F32)
    mid = rest.astype(BF16)
    low = (rest - mid.astype(F32)).astype(BF16)
    return high, mid, low


def dot(a, b, dims):
    return lax.dot_general(a, b, (dims, ((), ())), preferred_element_type=F32)


SPAN_MOMENT_CHUNKS = 2
STEP = 8


def table_loads(sources, targets, sems, wall_count):
    for j, (source, target) in enumerate(zip(sources, targets)):
        at = lax.axis_index("wall") if j < wall_count else lax.axis_index("span")
        yield pltpu.make_async_copy(source.at[at], target, sems.at[j])


def wall_moment_kernel(x_hbm, *refs):
    sources, targets = refs[:7], refs[7:14]
    x_ref, pay_ref, other_ref, x_sems, t_sems = refs[14:]
    fields, planes, rows, _ = x_ref.shape

    loads = list(table_loads(sources, targets, t_sems, 3))
    copies = [pltpu.make_async_copy(x_hbm.at[f], x_ref.at[f], x_sems.at[f]) for f in range(fields)]
    loads[0].start()
    for copy in copies:
        copy.start()
    for load in loads[1:]:
        load.start()
    loads[0].wait()
    even = lax.axis_index("wall") % 2 == 0
    table = targets[0][...].T[:rows]
    right, left = table[:, 0:1], table[:, 1:2]
    for f in range(fields):
        copies[f].wait()
        for q in range(0, planes, STEP):
            at = slice(q, q + STEP)
            x = x_ref[f, at]
            pay_ref[0, f, at] = jnp.sum(x * right[None], axis=1)
            pay_ref[1, f, at] = jnp.sum(x * left[None], axis=1)
            first, last = x[:, 0, :], x[:, rows - 1, :]
            pay_ref[2, f, at] = jnp.where(even, last, first)
            other_ref[f, at] = jnp.where(even, first, last)
    for load in loads[1:]:
        load.wait()


def wall_merge_kernel(last, first_round, sent_ref, got_ref, extra_ref, *refs):
    if first_round:
        coef_ref, pay_ref, state_ref = refs
    else:
        old_ref, coef_ref, pay_ref, state_ref = refs
    coef = coef_ref[...]

    def c(j):
        return coef[:, j : j + 1]

    base = 0 if first_round else (16 if last else 8)
    got_r, got_l, halo = got_ref[0], got_ref[1], got_ref[2]
    for j, value in enumerate((c(base) * got_r, c(base + 1) * got_l, c(base + 6) * halo, c(base + 7) * halo)):
        state_ref[j] = value if first_round else old_ref[j] + value
    own_r = c(base + 2) * sent_ref[0] + c(base + 3) * got_r
    own_l = c(base + 4) * sent_ref[1] + c(base + 5) * got_l
    if last:
        pay_ref[0] = c(32) * own_l + c(33) * own_r
        pay_ref[1] = extra_ref[...]
    else:
        pay_ref[0] = own_r
        pay_ref[1] = own_l
        pay_ref[2] = extra_ref[...]


def wall_local_kernel(x_ref, table_ref, out_ref):
    fields, planes, block, lanes = x_ref.shape
    table = table_ref[...]
    pad = table.shape[1] - block
    d_high, d_mid, d_low = table[:block], table[block : 2 * block], table[2 * block :]
    lhs = jnp.concatenate([jnp.concatenate([d_high, d_high], axis=1), jnp.concatenate([d_mid, d_mid], axis=1)], axis=0)
    lhs2 = jnp.concatenate([d_high, d_low], axis=1)

    def stacked(a, b):
        return jnp.concatenate([a, a[:pad], b, b[:pad]], axis=0)

    for f in range(fields):
        flat = jnp.concatenate([x_ref[f, q] for q in range(planes)], axis=1)
        high, mid, low = split_parts(flat)
        main = dot(lhs, stacked(high, mid), ((1,), (0,)))
        rest = dot(lhs2, stacked(low, high), ((1,), (0,)))
        total = main[:block] + (main[block:] + rest)
        for q in range(planes):
            out_ref[f, q] = total[:, q * lanes : (q + 1) * lanes]


def wall_final_kernel(local_ref, metric_ref, old_ref, got_ref, coef_ref, table_ref, out_hbm, buffer, sems):
    fields, planes, block, _ = local_ref.shape
    coef = coef_ref[...]
    table = table_ref[...].T[:block]
    enter, leave = table[:, 2:3], table[:, 3:4]
    top = lax.broadcasted_iota(jnp.int32, (1, 8, 1), 1) == 0
    bottom = lax.broadcasted_iota(jnp.int32, (1, 8, 1), 1) == 7

    def c(j):
        return coef[:, j : j + 1]

    copies = []
    for f in range(fields):
        for q in range(0, planes, STEP):
            at = slice(q, q + STEP)
            got, halo = got_ref[0, f, at], got_ref[1, f, at]
            m, n = old_ref[0, f, at] + c(24) * got, old_ref[1, f, at] + c(25) * got
            first, last = old_ref[2, f, at] + c(30) * halo, old_ref[3, f, at] + c(31) * halo
            for lo, hi in ((0, 8), (8, block - 8), (block - 8, block)):
                total = local_ref[f, at, lo:hi] + enter[None, lo:hi] * m[:, None, :] + leave[None, lo:hi] * n[:, None, :]
                if lo == 0:
                    total = total + jnp.where(top, first[:, None, :], 0.0)
                if hi == block:
                    total = total + jnp.where(bottom, last[:, None, :], 0.0)
                buffer[f, at, lo:hi] = metric_ref[at, lo:hi] * total
            copies.append(pltpu.make_async_copy(buffer.at[f, at], out_hbm.at[f, at], sems.at[len(copies)]))
            copies[-1].start()
    for copy in copies:
        copy.wait()


def span_moment_kernel(x_ref, table_ref, pay_ref, other_ref):
    fields, planes, rows, columns = x_ref.shape
    even = lax.axis_index("span") % 2 == 0
    table = table_ref[...]
    for i in range(SPAN_MOMENT_CHUNKS):
        lines = fields * planes * rows // SPAN_MOMENT_CHUNKS
        at = slice(i * lines, (i + 1) * lines)
        flat = x_ref[...].reshape(fields * planes * rows, columns)[at]
        high, mid, low = split_parts(flat)
        main = dot(table[:16], jnp.concatenate([high, mid], axis=1), ((1,), (1,)))
        rest = dot(table[16:], jnp.concatenate([low, high], axis=1), ((1,), (1,)))
        total = main[:8] + (main[8:] + rest[:8])
        first, last = total[2:3], total[3:4]
        pay_ref[0:2, at] = total[0:2]
        pay_ref[2:3, at] = jnp.where(even, last, first)
        other_ref[:, at] = jnp.where(even, first, last)


def span_merge_kernel(sent_ref, got_ref, other_ref, coef_ref, pay_ref, state_ref):
    coef = coef_ref[...]

    def c(j):
        return coef[:, j : j + 1]

    got_r, got_l, halo = got_ref[0:1], got_ref[1:2], got_ref[2:3]
    for j, value in enumerate((c(0) * got_r, c(1) * got_l, c(6) * halo, c(7) * halo)):
        state_ref[j : j + 1] = value
    own_r = c(2) * sent_ref[0:1] + c(3) * got_r
    own_l = c(4) * sent_ref[1:2] + c(5) * got_l
    pay_ref[0:1] = c(16) * own_l + c(17) * own_r
    pay_ref[1:2] = other_ref[...]


def span_final_kernel(x_ref, metric_ref, old_ref, got_ref, coef_ref, table_ref, edge_ref, out_hbm, buffer, sems):
    fields, planes, rows, n = x_ref.shape
    coef = coef_ref[...]
    table = table_ref[...]
    d_high, d_low = table[:, :n], table[:, 2 * n :]
    weights = jnp.concatenate([table[:, : 2 * n], table[:, : 2 * n]], axis=0)
    weights2 = jnp.concatenate([d_high, d_low], axis=0)

    def c(j):
        return coef[:, j : j + 1]

    copies = []
    lines = planes * rows
    for f in range(fields):
        flat = x_ref[f].reshape(lines, n)
        high, mid, low = split_parts(flat)
        main = dot(jnp.concatenate([high, mid], axis=1), weights, ((1,), (0,)))
        rest = dot(jnp.concatenate([low, high], axis=1), weights2, ((1,), (0,)))
        line = slice(f * lines, (f + 1) * lines)
        got, halo, old = got_ref[0:1, line], got_ref[1:2, line], old_ref[:, line]
        state = jnp.concatenate(
            [old[0:1] + c(8) * got, old[1:2] + c(9) * got, old[2:3] + c(14) * halo, old[3:4] + c(15) * halo]
            + [jnp.zeros((4, lines), F32)]
        )
        s_high = state.astype(BF16).astype(F32)
        s_rest = state - s_high
        s_mid = s_rest.astype(BF16).astype(F32)
        s_low = s_rest - s_mid
        parts = jnp.concatenate([s_high, s_high, s_mid, s_high, s_mid, s_low], axis=0).astype(BF16)
        edge = dot(parts, edge_ref[...], ((0,), (0,)))
        total = main[:, :n] + (main[:, n:] + (rest + edge))
        buffer[f] = metric_ref[...] * total.reshape(planes, rows, n)
        copies.append(pltpu.make_async_copy(buffer.at[f], out_hbm.at[f], sems.at[f]))
        copies[-1].start()
    for copy in copies:
        copy.wait()


def slopes(conserved, wall_metric, span_metric):
    fields, planes, rows, columns = conserved.shape
    wall_pieces, span_pieces = lax.axis_size("wall"), lax.axis_size("span")
    wt = line_tables(rows * wall_pieces, wall_pieces)
    st = line_tables(columns * span_pieces, span_pieces)
    chunks = fields * planes // STEP
    lines = fields * planes * rows
    vmem = pl.BlockSpec(memory_space=pltpu.VMEM)
    hbm = pl.BlockSpec(memory_space=pltpu.HBM)

    def shape(*dims, dtype=F32):
        return jax.ShapeDtypeStruct(dims, dtype)

    def call(kernel, in_specs, out_specs, out_shape, micros, scratch=()):
        return pl.pallas_call(
            kernel,
            in_specs=in_specs,
            out_specs=out_specs,
            out_shape=out_shape,
            scratch_shapes=list(scratch),
            compiler_params=pltpu.CompilerParams(vmem_limit_bytes=VMEM_LIMIT),
            cost_estimate=pl.CostEstimate(flops=0, transcendentals=0, bytes_accessed=int(micros * 3.0e6)),
        )

    wall_rows = np.zeros((wall_pieces, 8, LANES), np.float32)
    for j, key in enumerate(("right", "left", "enter", "leave")):
        wall_rows[:, j, :rows] = wt[key]
    wall_diag = np.zeros((wall_pieces, 3 * rows, LANES), BF16)
    wall_diag[:, :, :rows] = np.concatenate(split_table(wt["diag"]), axis=1)
    span_diag = np.concatenate(split_table(np.swapaxes(st["diag"], 1, 2)), axis=2)
    pick = np.zeros((span_pieces, 4, columns))
    pick[:, 0], pick[:, 1] = st["right"], st["left"]
    pick[:, 2, 0] = 1.0
    pick[:, 3, columns - 1] = 1.0
    p_high, p_mid, p_low = split_table(pick)
    span_pick = np.zeros((span_pieces, 32, 2 * columns), BF16)
    span_pick[:, 0:4] = np.concatenate([p_high, p_high], axis=2)
    span_pick[:, 8:12] = np.concatenate([p_mid, p_mid], axis=2)
    span_pick[:, 16:20] = np.concatenate([p_high, p_low], axis=2)
    spread = np.zeros((span_pieces, 8, columns))
    spread[:, 0], spread[:, 1] = st["enter"], st["leave"]
    spread[:, 2, 0] = 1.0
    spread[:, 3, columns - 1] = 1.0
    e_high, e_mid, e_low = split_table(spread)
    span_edge = np.concatenate([e_high, e_mid, e_high, e_low, e_mid, e_high], axis=1)

    def spread_coefficients(t, pieces):
        c = doubling_coefficients(t, pieces)
        out = np.zeros((pieces, 1, LANES), np.float32)
        out[:, 0, : c.shape[1]] = c
        return out

    tables = [wall_rows, wall_diag, spread_coefficients(wt, wall_pieces)]
    tables += [span_diag, span_pick, span_edge, spread_coefficients(st, span_pieces)]
    tables = [pltpu.with_memory_space_constraint(jnp.asarray(t), pltpu.HBM) for t in tables]
    grid_values = pltpu.with_memory_space_constraint(conserved, pltpu.HBM)

    state = shape(4, fields, planes, columns)
    moment = shape(3, fields, planes, columns)
    out = call(
        wall_moment_kernel,
        [hbm] * 8,
        [vmem] * 10,
        [shape(*t.shape[1:], dtype=t.dtype) for t in tables]
        + [shape(*conserved.shape), moment, shape(fields, planes, columns)],
        2.5,
        [pltpu.SemaphoreType.DMA((fields,)), pltpu.SemaphoreType.DMA((len(tables),))],
    )(grid_values, *tables)
    w_rows, w_diag, w_coef, s_diag, s_pick, s_edge, s_coef, x, pay_w, other_w = out

    def swap(flip, pieces):
        return [(k, k ^ flip) for k in range(pieces)]

    got_w = lax.ppermute(pay_w, "wall", swap(1, wall_pieces))

    pay_s, other_s = call(
        span_moment_kernel, [vmem] * 2, [vmem] * 2, [shape(3, lines), shape(1, lines)], 3.4
    )(x, s_pick)
    pay_w, state_w = call(
        functools.partial(wall_merge_kernel, False, True), [vmem] * 4, [vmem] * 2, [moment, state], 0.2
    )(pay_w, got_w, other_w, w_coef)
    got_w = lax.ppermute(pay_w, "wall", swap(3, wall_pieces))
    got_s = lax.ppermute(pay_s, "span", swap(1, span_pieces))
    halo = got_w[2]

    local_w = call(wall_local_kernel, [vmem] * 2, vmem, shape(*conserved.shape), 3.5)(x, w_diag)

    pay_s, state_s = call(
        span_merge_kernel, [vmem] * 4, [vmem] * 2, [shape(2, lines), shape(4, lines)], 0.2
    )(pay_s, got_s, other_s, s_coef)
    got_s = lax.ppermute(pay_s, "span", swap(3, span_pieces))

    pay_w, state_w = call(
        functools.partial(wall_merge_kernel, False, False), [vmem] * 5, [vmem] * 2, [moment, state], 0.2
    )(pay_w, got_w, halo, state_w, w_coef)
    got_w = lax.ppermute(pay_w, "wall", swap(4, wall_pieces))

    pay_w, state_w = call(
        functools.partial(wall_merge_kernel, True, False), [vmem] * 5, [vmem] * 2,
        [shape(2, fields, planes, columns), state], 0.2,
    )(pay_w, got_w, halo, state_w, w_coef)
    got_w = lax.ppermute(pay_w, "wall", swap(12, wall_pieces))

    buffers = [pltpu.VMEM(conserved.shape, F32), pltpu.SemaphoreType.DMA((chunks,))]
    span_slope = call(
        span_final_kernel, [vmem] * 7, hbm, shape(*conserved.shape), 6.0, buffers
    )(x, span_metric, state_s, got_s, s_coef, s_diag, s_edge)
    wall_slope = call(
        wall_final_kernel, [vmem] * 6, hbm, shape(*conserved.shape), 4.0, buffers
    )(local_w, wall_metric, state_w, got_w, w_coef, w_rows)
    return (wall_slope, span_slope)


def solution(mesh):
    in_specs = (
        P(None, "stream", "wall", "span"),
        P("stream", "wall", "span"),
        P("stream", "wall", "span"),
    )
    out_specs = (P(None, "stream", "wall", "span"), P(None, "stream", "wall", "span"))
    return jax.shard_map(slopes, mesh=mesh, in_specs=in_specs, out_specs=out_specs, check_vma=False)
```

```python
import functools

import jax
import jax.numpy as jnp
import numpy as np
from jax import lax
from jax.experimental import pallas as pl
from jax.experimental.pallas import tpu as pltpu
from jax.sharding import PartitionSpec as P


F32 = jnp.float32
BF16 = jnp.bfloat16
band_alpha = 0.4995
LANES = 128
VMEM_LIMIT = 24 * 2**20


def line_coefficients(length_all):
    lower_band = np.full(length_all, band_alpha)
    lower_band[1] = 0.25
    lower_band[length_all - 2] = 0.25
    lower_band[0] = 0.0
    lower_band[length_all - 1] = 0.0
    scales = np.zeros(length_all)
    pivots = np.zeros(length_all)
    previous = 0.0
    for row_idx in range(length_all):
        scales[row_idx] = 1.0 / (1.0 - lower_band[row_idx] * previous)
        pivots[row_idx] = lower_band[row_idx] * scales[row_idx]
        previous = pivots[row_idx]
    near_coef = (band_alpha + 2.0) / 3.0
    far_coef = (4.0 * band_alpha - 1.0) / 12.0
    weights = np.zeros((5, length_all))
    weights[:, :] = np.array([-far_coef, -near_coef, 0.0, near_coef, far_coef])[:, None]
    weights[:, 1] = [0.0, -0.75, 0.0, 0.75, 0.0]
    weights[:, length_all - 2] = [0.0, -0.75, 0.0, 0.75, 0.0]
    weights[:, 0] = [0.0, 0.0, -1.5, 2.0, -0.5]
    weights[:, length_all - 1] = [0.5, -2.0, 1.5, 0.0, 0.0]
    return (lower_band, scales, pivots, weights)


@functools.lru_cache(maxsize=None)
def line_tables(length_all, pieces):
    block = length_all // pieces
    lower_band, scales, pivots, weights = line_coefficients(length_all)

    def solve(rows):
        out = np.zeros_like(rows)
        running = np.zeros(rows.shape[1])
        for i in range(length_all):
            running = (rows[i] - lower_band[i] * running) * scales[i]
            out[i] = running
        running = np.zeros(rows.shape[1])
        for i in range(length_all - 1, -1, -1):
            running = out[i] - pivots[i] * running
            out[i] = running
        return out

    stencil = np.zeros((length_all, length_all))
    for k in range(5):
        for g in range(length_all):
            if 0 <= g + k - 2 < length_all:
                stencil[g, g + k - 2] = weights[k, g]
    whole = solve(stencil)
    unit = np.zeros((length_all, 2 * pieces))
    for k in range(pieces):
        unit[k * block, k] = 1.0
        unit[k * block + block - 1, pieces + k] = 1.0
    inverse = solve(unit)
    t = {
        "diag": np.zeros((pieces, block, block)),
        "enter": np.zeros((pieces, block)),
        "leave": np.zeros((pieces, block)),
        "right": np.zeros((pieces, block)),
        "left": np.zeros((pieces, block)),
        "first": np.zeros(pieces),
        "last": np.zeros(pieces),
        "pass_right": np.ones(pieces),
        "pass_left": np.ones(pieces),
    }
    for k in range(pieces):
        lo, hi = k * block, k * block + block
        t["diag"][k] = whole[lo:hi, lo:hi]
        t["enter"][k] = inverse[lo:hi, k] / inverse[lo, k]
        t["leave"][k] = inverse[lo:hi, pieces + k] / inverse[hi - 1, pieces + k]
        if k < pieces - 1:
            t["pass_right"][k] = inverse[hi, k] / inverse[lo, k]
        if k > 0:
            t["pass_left"][k] = inverse[lo - 1, pieces + k] / inverse[hi - 1, pieces + k]
    for k in range(pieces):
        lo, hi = k * block, k * block + block
        if k < pieces - 1:
            t["right"][k] = whole[hi + 1, lo:hi] / t["enter"][k + 1][1]
        if k > 0:
            t["left"][k] = whole[lo - 2, lo:hi] / t["leave"][k - 1][block - 2]
    for k in range(pieces):
        lo, hi = k * block, k * block + block
        if k > 0:
            t["first"][k] = whole[lo, lo - 1] - t["right"][k - 1][block - 1]
        if k < pieces - 1:
            t["last"][k] = whole[hi - 1, hi] - t["left"][k + 1][0]
    return t


def doubling_coefficients(t, pieces):
    rounds = pieces.bit_length() - 1
    right, left = t["pass_right"], t["pass_left"]
    coef = np.zeros((pieces, rounds, 8))
    for r in range(rounds):
        half = 1 << r
        for k in range(pieces):
            base = k // half * half
            inside = slice(base, base + half)
            if (k // half) % 2:
                other = slice(base - half, base)
                coef[k, r, :6] = [np.prod(right[base:k]), 0.0, 1.0, np.prod(right[inside]), np.prod(left[other]), 1.0]
            else:
                other = slice(base + half, base + 2 * half)
                coef[k, r, :6] = [0.0, np.prod(left[k + 1 : base + half]), np.prod(right[other]), 1.0, 1.0, np.prod(left[inside])]
    for k in range(pieces):
        if k > 0:
            coef[k, halo_round(k - 1), 6] = t["first"][k]
        if k < pieces - 1:
            coef[k, halo_round(k), 7] = t["last"][k]
    pick = np.array([[float(k >= pieces // 2), float(k < pieces // 2)] for k in range(pieces)])
    return np.concatenate([coef.reshape(pieces, -1), pick], axis=1)


def halo_round(k):
    if k % 2 == 0:
        return 0
    if k % 4 == 1:
        return 1
    return 2 if k % 8 == 3 else 3


def split_table(x):
    x = np.asarray(x, np.float32)
    high = x.astype(BF16)
    rest = x - high.astype(np.float32)
    mid = rest.astype(BF16)
    low = (rest - mid.astype(np.float32)).astype(BF16)
    return high, mid, low


def split_parts(x):
    high = x.astype(BF16)
    rest = x - high.astype(F32)
    mid = rest.astype(BF16)
    low = (rest - mid.astype(F32)).astype(BF16)
    return high, mid, low


def dot(a, b, dims):
    return lax.dot_general(a, b, (dims, ((), ())), preferred_element_type=F32)


READY = ((0,), (1,))
STEP = 8


def table_loads(sources, targets, sems, wall_count):
    for j, (source, target) in enumerate(zip(sources, targets)):
        at = lax.axis_index("wall") if j < wall_count else lax.axis_index("span")
        yield pltpu.make_async_copy(source.at[at], target, sems.at[j])


def wall_moment_kernel(x_hbm, *refs):
    sources, targets = refs[:7], refs[7:14]
    x_ref, pay_ref, other_ref, x_sems, t_sems = refs[14:]
    fields, planes, rows, _ = x_ref.shape

    loads = list(table_loads(sources, targets, t_sems, 3))
    pieces = [(f, slice(q, q + STEP)) for f in range(fields) for q in range(0, planes, STEP)]
    copies = [pltpu.make_async_copy(x_hbm.at[p], x_ref.at[p], x_sems.at[i]) for i, p in enumerate(pieces)]
    loads[0].start()
    for copy in copies:
        copy.start()
    for load in loads[1:]:
        load.start()
    loads[0].wait()
    even = lax.axis_index("wall") % 2 == 0
    table = targets[0][...].T[:rows]
    right, left = table[:, 0:1], table[:, 1:2]
    for copy, (f, at) in zip(copies, pieces):
        copy.wait()
        x = x_ref[f, at]
        pay_ref[0, f, at] = jnp.sum(x * right[None], axis=1)
        pay_ref[1, f, at] = jnp.sum(x * left[None], axis=1)
        first, last = x[:, 0, :], x[:, rows - 1, :]
        pay_ref[2, f, at] = jnp.where(even, last, first)
        other_ref[f, at] = jnp.where(even, first, last)
    for load in loads[1:]:
        load.wait()


def wall_merge_kernel(last, first_round, sent_ref, got_ref, extra_ref, *refs):
    if first_round:
        coef_ref, pay_ref, state_ref = refs
    else:
        old_ref, coef_ref, pay_ref, state_ref = refs
    coef = coef_ref[...]

    def c(j):
        return coef[:, j : j + 1]

    base = 0 if first_round else (16 if last else 8)
    got_r, got_l, halo = got_ref[0], got_ref[1], got_ref[2]
    for j, value in enumerate((c(base) * got_r, c(base + 1) * got_l, c(base + 6) * halo, c(base + 7) * halo)):
        state_ref[j] = value if first_round else old_ref[j] + value
    own_r = c(base + 2) * sent_ref[0] + c(base + 3) * got_r
    own_l = c(base + 4) * sent_ref[1] + c(base + 5) * got_l
    if last:
        pay_ref[0] = c(32) * own_l + c(33) * own_r
        pay_ref[1] = extra_ref[...]
    else:
        pay_ref[0] = own_r
        pay_ref[1] = own_l
        pay_ref[2] = extra_ref[...]


def wall_local_kernel(high_ref, mid_ref, low_ref, table_ref, metric_a, metric_b, out_ref, metric_a_ref, metric_b_ref, sems):
    fields, planes, block, lanes = out_ref.shape
    loads = [pltpu.make_async_copy(metric_a, metric_a_ref, sems.at[0]), pltpu.make_async_copy(metric_b, metric_b_ref, sems.at[1])]
    for load in loads:
        load.start()
    table = table_ref[...].astype(F32)
    lane = lax.broadcasted_iota(jnp.int32, table.shape, 1)
    again = pltpu.roll(table, block, 1)

    def beside(a, b):
        return jnp.concatenate([jnp.where(lane[:block] < block, a[0], b[1]), b[1]], axis=1)[:, : 2 * block].astype(BF16)

    parts = [(table[j * block : (j + 1) * block], again[j * block : (j + 1) * block]) for j in range(3)]
    lhs = jnp.concatenate([beside(parts[0], parts[0]), beside(parts[1], parts[1])], axis=0)
    lhs2 = beside(parts[0], parts[2])

    for f in range(fields):
        high, mid, low = (
            jnp.concatenate([ref[f, q] for q in range(planes)], axis=1) for ref in (high_ref, mid_ref, low_ref)
        )
        main = dot(lhs, jnp.concatenate([high, mid], axis=0), ((1,), (0,)))
        rest = dot(lhs2, jnp.concatenate([low, high], axis=0), ((1,), (0,)))
        total = main[:block] + (main[block:] + rest)
        for q in range(planes):
            out_ref[f, q] = total[:, q * lanes : (q + 1) * lanes]
    for load in loads:
        load.wait()


def wall_final_kernel(
    local_ref, metric_ref, old_ref, got_ref, coef_ref, table_ref, tail_ref, span_in, out_hbm, span_hbm, buffer, sems
):
    fields, planes, block, _ = local_ref.shape
    coef = coef_ref[...]
    table = table_ref[...].T[:block]
    enter, leave = table[:, 2:3], table[:, 3:4]
    top = lax.broadcasted_iota(jnp.int32, (1, 8, 1), 1) == 0
    bottom = lax.broadcasted_iota(jnp.int32, (1, 8, 1), 1) == 7

    def c(j):
        return coef[:, j : j + 1]

    copies = [pltpu.make_async_copy(tail_ref, span_hbm.at[fields - 1], sems.at[0])]
    copies[0].start()
    for f in range(fields):
        for q in range(0, planes, STEP):
            at = slice(q, q + STEP)
            got, halo = got_ref[0, f, at], got_ref[1, f, at]
            m, n = old_ref[0, f, at] + c(24) * got, old_ref[1, f, at] + c(25) * got
            first, last = old_ref[2, f, at] + c(30) * halo, old_ref[3, f, at] + c(31) * halo
            for lo, hi in ((0, 8), (8, block - 8), (block - 8, block)):
                total = local_ref[f, at, lo:hi] + enter[None, lo:hi] * m[:, None, :] + leave[None, lo:hi] * n[:, None, :]
                if lo == 0:
                    total = total + jnp.where(top, first[:, None, :], 0.0)
                if hi == block:
                    total = total + jnp.where(bottom, last[:, None, :], 0.0)
                buffer[f, at, lo:hi] = metric_ref[at, lo:hi] * total
            copies.append(pltpu.make_async_copy(buffer.at[f, at], out_hbm.at[f, at], sems.at[len(copies)]))
            copies[-1].start()
    for copy in copies:
        copy.wait()


def span_moment_kernel(x_ref, table_ref, pay_ref, other_ref, high_ref, mid_ref, low_ref):
    fields, planes, rows, columns = x_ref.shape
    even = lax.axis_index("span") % 2 == 0
    table = table_ref[...]
    lines = planes * rows
    for f in range(fields):
        at = slice(f * lines, (f + 1) * lines)
        high, mid, low = split_parts(x_ref[f].reshape(lines, columns))
        for ref, part in ((high_ref, high), (mid_ref, mid), (low_ref, low)):
            ref[f] = part.reshape(planes, rows, columns)
        main = dot(table[:16], jnp.concatenate([high, mid], axis=1), ((1,), (1,)))
        rest = dot(table[16:], jnp.concatenate([low, high], axis=1), ((1,), (1,)))
        total = main[:8] + (main[8:] + rest[:8])
        first, last = total[2:3], total[3:4]
        pay_ref[0:2, at] = total[0:2]
        pay_ref[2:3, at] = jnp.where(even, last, first)
        other_ref[:, at] = jnp.where(even, first, last)


def span_matrices(table):
    n = table.shape[0]
    return (
        jnp.concatenate([table[:, : 2 * n], table[:, : 2 * n]], axis=0),
        jnp.concatenate([table[:, :n], table[:, 2 * n :]], axis=0),
    )


def span_product(weights, high, mid, low):
    n = high.shape[1]
    main = dot(jnp.concatenate([high, mid], axis=1), weights[0], ((1,), (0,)))
    rest = dot(jnp.concatenate([low, high], axis=1), weights[1], ((1,), (0,)))
    return main[:, :n], main[:, n:] + rest


def span_local_kernel(start, high_ref, mid_ref, low_ref, table_ref, out_ref):
    count, planes, rows, n = out_ref.shape
    weights = span_matrices(table_ref[...])
    for j in range(count):
        parts = (ref[start + j].reshape(planes * rows, n) for ref in (high_ref, mid_ref, low_ref))
        a, b = span_product(weights, *parts)
        out_ref[j] = (a + b).reshape(planes, rows, n)


def span_merge_kernel(sent_ref, got_ref, other_ref, coef_ref, pay_ref, state_ref):
    coef = coef_ref[...]

    def c(j):
        return coef[:, j : j + 1]

    got_r, got_l, halo = got_ref[0:1], got_ref[1:2], got_ref[2:3]
    for j, value in enumerate((c(0) * got_r, c(1) * got_l, c(6) * halo, c(7) * halo)):
        state_ref[j : j + 1] = value
    own_r = c(2) * sent_ref[0:1] + c(3) * got_r
    own_l = c(4) * sent_ref[1:2] + c(5) * got_l
    pay_ref[0:1] = c(16) * own_l + c(17) * own_r
    pay_ref[1:2] = other_ref[...]


def span_final_kernel(ready, high_ref, mid_ref, low_ref, metric_ref, old_ref, got_ref, coef_ref, table_ref, edge_ref, *refs):
    locals_ref = refs[: len(ready)]
    out_hbm, tail_ref, buffer, sems = refs[len(ready) :]
    fields, planes, rows, n = high_ref.shape
    coef = coef_ref[...]
    weights = span_matrices(table_ref[...])

    def c(j):
        return coef[:, j : j + 1]

    copies = []
    lines = planes * rows
    own = {f: (ref, j) for ref, group in zip(locals_ref, ready) for j, f in enumerate(group)}
    for f in range(fields):
        line = slice(f * lines, (f + 1) * lines)
        got, halo, old = got_ref[0:1, line], got_ref[1:2, line], old_ref[:, line]
        state = jnp.concatenate(
            [old[0:1] + c(8) * got, old[1:2] + c(9) * got, old[2:3] + c(14) * halo, old[3:4] + c(15) * halo]
            + [jnp.zeros((4, lines), F32)]
        )
        s_high = state.astype(BF16).astype(F32)
        s_rest = state - s_high
        s_mid = s_rest.astype(BF16).astype(F32)
        s_low = s_rest - s_mid
        parts = jnp.concatenate([s_high, s_high, s_mid, s_high, s_mid, s_low], axis=0).astype(BF16)
        edge = dot(parts, edge_ref[...], ((0,), (0,)))
        if f in own:
            ref, j = own[f]
            total = ref[j].reshape(lines, n) + edge
        else:
            a, b = span_product(weights, *(ref[f].reshape(lines, n) for ref in (high_ref, mid_ref, low_ref)))
            total = a + (b + edge)
        total = metric_ref[...] * total.reshape(planes, rows, n)
        if f == fields - 1:
            tail_ref[...] = total
        else:
            buffer[f] = total
            copies.append(pltpu.make_async_copy(buffer.at[f], out_hbm.at[f], sems.at[f]))
            copies[-1].start()
    for copy in copies:
        copy.wait()


def slopes(conserved, wall_metric, span_metric):
    fields, planes, rows, columns = conserved.shape
    wall_pieces, span_pieces = lax.axis_size("wall"), lax.axis_size("span")
    wt = line_tables(rows * wall_pieces, wall_pieces)
    st = line_tables(columns * span_pieces, span_pieces)
    chunks = fields * planes // STEP
    lines = fields * planes * rows
    vmem = pl.BlockSpec(memory_space=pltpu.VMEM)
    hbm = pl.BlockSpec(memory_space=pltpu.HBM)

    def shape(*dims, dtype=F32):
        return jax.ShapeDtypeStruct(dims, dtype)

    def call(kernel, in_specs, out_specs, out_shape, micros, scratch=(), aliases=None):
        return pl.pallas_call(
            kernel,
            in_specs=in_specs,
            out_specs=out_specs,
            out_shape=out_shape,
            scratch_shapes=list(scratch),
            input_output_aliases=aliases or {},
            compiler_params=pltpu.CompilerParams(vmem_limit_bytes=VMEM_LIMIT),
            cost_estimate=pl.CostEstimate(flops=0, transcendentals=0, bytes_accessed=int(micros * 3.0e6)),
        )

    wall_rows = np.zeros((wall_pieces, 8, LANES), np.float32)
    for j, key in enumerate(("right", "left", "enter", "leave")):
        wall_rows[:, j, :rows] = wt[key]
    wall_diag = np.zeros((wall_pieces, 3 * rows, LANES), BF16)
    wall_diag[:, :, :rows] = np.concatenate(split_table(wt["diag"]), axis=1)
    span_diag = np.concatenate(split_table(np.swapaxes(st["diag"], 1, 2)), axis=2)
    pick = np.zeros((span_pieces, 4, columns))
    pick[:, 0], pick[:, 1] = st["right"], st["left"]
    pick[:, 2, 0] = 1.0
    pick[:, 3, columns - 1] = 1.0
    p_high, p_mid, p_low = split_table(pick)
    span_pick = np.zeros((span_pieces, 32, 2 * columns), BF16)
    span_pick[:, 0:4] = np.concatenate([p_high, p_high], axis=2)
    span_pick[:, 8:12] = np.concatenate([p_mid, p_mid], axis=2)
    span_pick[:, 16:20] = np.concatenate([p_high, p_low], axis=2)
    spread = np.zeros((span_pieces, 8, columns))
    spread[:, 0], spread[:, 1] = st["enter"], st["leave"]
    spread[:, 2, 0] = 1.0
    spread[:, 3, columns - 1] = 1.0
    e_high, e_mid, e_low = split_table(spread)
    span_edge = np.concatenate([e_high, e_mid, e_high, e_low, e_mid, e_high], axis=1)

    def spread_coefficients(t, pieces):
        c = doubling_coefficients(t, pieces)
        out = np.zeros((pieces, 1, LANES), np.float32)
        out[:, 0, : c.shape[1]] = c
        return out

    tables = [wall_rows, wall_diag, spread_coefficients(wt, wall_pieces)]
    tables += [span_diag, span_pick, span_edge, spread_coefficients(st, span_pieces)]
    tables = [pltpu.with_memory_space_constraint(jnp.asarray(t), pltpu.HBM) for t in tables]
    grid_values = pltpu.with_memory_space_constraint(conserved, pltpu.HBM)

    state = shape(4, fields, planes, columns)
    moment = shape(3, fields, planes, columns)
    out = call(
        wall_moment_kernel,
        [hbm] * 8,
        [vmem] * 10,
        [shape(*t.shape[1:], dtype=t.dtype) for t in tables]
        + [shape(*conserved.shape), moment, shape(fields, planes, columns)],
        2.5,
        [pltpu.SemaphoreType.DMA((chunks,)), pltpu.SemaphoreType.DMA((len(tables),))],
    )(grid_values, *tables)
    w_rows, w_diag, w_coef, s_diag, s_pick, s_edge, s_coef, x, pay_w, other_w = out

    def swap(flip, pieces):
        return [(k, k ^ flip) for k in range(pieces)]

    got_w = lax.ppermute(pay_w, "wall", swap(1, wall_pieces))

    part = shape(*conserved.shape, dtype=BF16)
    pay_s, other_s, *parts = call(
        span_moment_kernel, [vmem] * 2, [vmem] * 5, [shape(3, lines), shape(1, lines)] + [part] * 3, 2.1
    )(x, s_pick)
    got_s = lax.ppermute(pay_s, "span", swap(1, span_pieces))

    pay_w, state_w = call(
        functools.partial(wall_merge_kernel, False, True), [vmem] * 4, [vmem] * 2, [moment, state], 0.2
    )(pay_w, got_w, other_w, w_coef)
    got_w = lax.ppermute(pay_w, "wall", swap(3, wall_pieces))
    halo = got_w[2]

    local_w, span_metric, wall_metric = call(
        wall_local_kernel, [vmem] * 4 + [hbm] * 2, [vmem] * 3,
        [shape(*conserved.shape)] + [shape(*wall_metric.shape)] * 2, 1.7,
        [pltpu.SemaphoreType.DMA((2,))],
    )(*parts, w_diag, *(pltpu.with_memory_space_constraint(m, pltpu.HBM) for m in (span_metric, wall_metric)))

    def span_local(group):
        return call(
            functools.partial(span_local_kernel, group[0]), [vmem] * 4, vmem,
            shape(len(group), planes, rows, columns), 0.6 * len(group),
        )(*parts, s_diag)

    own_s = [span_local(group) for group in READY]

    pay_s, state_s = call(
        span_merge_kernel, [vmem] * 4, [vmem] * 2, [shape(2, lines), shape(4, lines)], 0.2
    )(pay_s, got_s, other_s, s_coef)
    got_s = lax.ppermute(pay_s, "span", swap(3, span_pieces))

    pay_w, state_w = call(
        functools.partial(wall_merge_kernel, False, False), [vmem] * 5, [vmem] * 2, [moment, state], 0.2
    )(pay_w, got_w, halo, state_w, w_coef)
    got_w = lax.ppermute(pay_w, "wall", swap(4, wall_pieces))

    pay_w, state_w = call(
        functools.partial(wall_merge_kernel, True, False), [vmem] * 5, [vmem] * 2,
        [shape(2, fields, planes, columns), state], 0.2,
    )(pay_w, got_w, halo, state_w, w_coef)
    got_w = lax.ppermute(pay_w, "wall", swap(12, wall_pieces))

    span_slope, tail = call(
        functools.partial(span_final_kernel, READY), [vmem] * (9 + len(READY)), [hbm, vmem],
        [shape(*conserved.shape), shape(planes, rows, columns)], 3.0,
        [pltpu.VMEM((fields - 1, planes, rows, columns), F32), pltpu.SemaphoreType.DMA((fields,))],
    )(*parts, span_metric, state_s, got_s, s_coef, s_diag, s_edge, *own_s)
    wall_slope, span_slope = call(
        wall_final_kernel, [vmem] * 7 + [hbm], [hbm] * 2, [shape(*conserved.shape)] * 2, 2.4,
        [pltpu.VMEM(conserved.shape, F32), pltpu.SemaphoreType.DMA((chunks + 1,))], {7: 1},
    )(local_w, wall_metric, state_w, got_w, w_coef, w_rows, tail, span_slope)
    return (wall_slope, span_slope)


def solution(mesh):
    in_specs = (
        P(None, "stream", "wall", "span"),
        P("stream", "wall", "span"),
        P("stream", "wall", "span"),
    )
    out_specs = (P(None, "stream", "wall", "span"), P(None, "stream", "wall", "span"))
    return jax.shard_map(slopes, mesh=mesh, in_specs=in_specs, out_specs=out_specs, check_vma=False)
```

```python
import functools

import jax
import jax.numpy as jnp
import numpy as np
from jax import lax
from jax.experimental import pallas as pl
from jax.experimental.pallas import tpu as pltpu
from jax.sharding import PartitionSpec as P


F32 = jnp.float32
BF16 = jnp.bfloat16
band_alpha = 0.4995
LANES = 128
VMEM_LIMIT = 24 * 2**20


def line_coefficients(length_all):
    lower_band = np.full(length_all, band_alpha)
    lower_band[1] = 0.25
    lower_band[length_all - 2] = 0.25
    lower_band[0] = 0.0
    lower_band[length_all - 1] = 0.0
    scales = np.zeros(length_all)
    pivots = np.zeros(length_all)
    previous = 0.0
    for row_idx in range(length_all):
        scales[row_idx] = 1.0 / (1.0 - lower_band[row_idx] * previous)
        pivots[row_idx] = lower_band[row_idx] * scales[row_idx]
        previous = pivots[row_idx]
    near_coef = (band_alpha + 2.0) / 3.0
    far_coef = (4.0 * band_alpha - 1.0) / 12.0
    weights = np.zeros((5, length_all))
    weights[:, :] = np.array([-far_coef, -near_coef, 0.0, near_coef, far_coef])[:, None]
    weights[:, 1] = [0.0, -0.75, 0.0, 0.75, 0.0]
    weights[:, length_all - 2] = [0.0, -0.75, 0.0, 0.75, 0.0]
    weights[:, 0] = [0.0, 0.0, -1.5, 2.0, -0.5]
    weights[:, length_all - 1] = [0.5, -2.0, 1.5, 0.0, 0.0]
    return (lower_band, scales, pivots, weights)


@functools.lru_cache(maxsize=None)
def line_tables(length_all, pieces):
    block = length_all // pieces
    lower_band, scales, pivots, weights = line_coefficients(length_all)

    def solve(rows):
        out = np.zeros_like(rows)
        running = np.zeros(rows.shape[1])
        for i in range(length_all):
            running = (rows[i] - lower_band[i] * running) * scales[i]
            out[i] = running
        running = np.zeros(rows.shape[1])
        for i in range(length_all - 1, -1, -1):
            running = out[i] - pivots[i] * running
            out[i] = running
        return out

    stencil = np.zeros((length_all, length_all))
    for k in range(5):
        for g in range(length_all):
            if 0 <= g + k - 2 < length_all:
                stencil[g, g + k - 2] = weights[k, g]
    whole = solve(stencil)
    unit = np.zeros((length_all, 2 * pieces))
    for k in range(pieces):
        unit[k * block, k] = 1.0
        unit[k * block + block - 1, pieces + k] = 1.0
    inverse = solve(unit)
    t = {
        "diag": np.zeros((pieces, block, block)),
        "enter": np.zeros((pieces, block)),
        "leave": np.zeros((pieces, block)),
        "right": np.zeros((pieces, block)),
        "left": np.zeros((pieces, block)),
        "first": np.zeros(pieces),
        "last": np.zeros(pieces),
        "pass_right": np.ones(pieces),
        "pass_left": np.ones(pieces),
    }
    for k in range(pieces):
        lo, hi = k * block, k * block + block
        t["diag"][k] = whole[lo:hi, lo:hi]
        t["enter"][k] = inverse[lo:hi, k] / inverse[lo, k]
        t["leave"][k] = inverse[lo:hi, pieces + k] / inverse[hi - 1, pieces + k]
        if k < pieces - 1:
            t["pass_right"][k] = inverse[hi, k] / inverse[lo, k]
        if k > 0:
            t["pass_left"][k] = inverse[lo - 1, pieces + k] / inverse[hi - 1, pieces + k]
    for k in range(pieces):
        lo, hi = k * block, k * block + block
        if k < pieces - 1:
            t["right"][k] = whole[hi + 1, lo:hi] / t["enter"][k + 1][1]
        if k > 0:
            t["left"][k] = whole[lo - 2, lo:hi] / t["leave"][k - 1][block - 2]
    for k in range(pieces):
        lo, hi = k * block, k * block + block
        if k > 0:
            t["first"][k] = whole[lo, lo - 1] - t["right"][k - 1][block - 1]
        if k < pieces - 1:
            t["last"][k] = whole[hi - 1, hi] - t["left"][k + 1][0]
    return t


def doubling_coefficients(t, pieces):
    rounds = pieces.bit_length() - 1
    right, left = t["pass_right"], t["pass_left"]
    coef = np.zeros((pieces, rounds, 8))
    for r in range(rounds):
        half = 1 << r
        for k in range(pieces):
            base = k // half * half
            inside = slice(base, base + half)
            if (k // half) % 2:
                other = slice(base - half, base)
                coef[k, r, :6] = [np.prod(right[base:k]), 0.0, 1.0, np.prod(right[inside]), np.prod(left[other]), 1.0]
            else:
                other = slice(base + half, base + 2 * half)
                coef[k, r, :6] = [0.0, np.prod(left[k + 1 : base + half]), np.prod(right[other]), 1.0, 1.0, np.prod(left[inside])]
    for k in range(pieces):
        if k > 0:
            coef[k, halo_round(k - 1), 6] = t["first"][k]
        if k < pieces - 1:
            coef[k, halo_round(k), 7] = t["last"][k]
    pick = np.array([[float(k >= pieces // 2), float(k < pieces // 2)] for k in range(pieces)])
    return np.concatenate([coef.reshape(pieces, -1), pick], axis=1)


def halo_round(k):
    if k % 2 == 0:
        return 0
    if k % 4 == 1:
        return 1
    return 2 if k % 8 == 3 else 3


def split_table(x):
    x = np.asarray(x, np.float32)
    high = x.astype(BF16)
    rest = x - high.astype(np.float32)
    mid = rest.astype(BF16)
    low = (rest - mid.astype(np.float32)).astype(BF16)
    return high, mid, low


def split_parts(x):
    high = x.astype(BF16)
    rest = x - high.astype(F32)
    mid = rest.astype(BF16)
    low = (rest - mid.astype(F32)).astype(BF16)
    return high, mid, low


def dot(a, b, dims):
    return lax.dot_general(a, b, (dims, ((), ())), preferred_element_type=F32)


READY = ((0, 1),)
SPAN_ROWS = 1536
STEP = 8


def table_loads(sources, targets, sems, wall_count):
    for j, (source, target) in enumerate(zip(sources, targets)):
        at = lax.axis_index("wall") if j < wall_count else lax.axis_index("span")
        yield pltpu.make_async_copy(source.at[at], target, sems.at[j])


def wall_moment_kernel(x_hbm, *refs):
    sources, targets = refs[:7], refs[7:14]
    x_ref, pay_ref, other_ref, x_sems, t_sems = refs[14:]
    fields, planes, rows, _ = x_ref.shape

    loads = list(table_loads(sources, targets, t_sems, 3))
    pieces = [(f, slice(q, q + STEP)) for f in range(fields) for q in range(0, planes, STEP)]
    copies = [pltpu.make_async_copy(x_hbm.at[p], x_ref.at[p], x_sems.at[i]) for i, p in enumerate(pieces)]
    loads[0].start()
    for copy in copies:
        copy.start()
    for load in loads[1:]:
        load.start()
    loads[0].wait()
    even = lax.axis_index("wall") % 2 == 0
    table = targets[0][...].T[:rows]
    right, left = table[:, 0:1], table[:, 1:2]
    for copy, (f, at) in zip(copies, pieces):
        copy.wait()
        x = x_ref[f, at]
        pay_ref[0, f, at] = jnp.sum(x * right[None], axis=1)
        pay_ref[1, f, at] = jnp.sum(x * left[None], axis=1)
        first, last = x[:, 0, :], x[:, rows - 1, :]
        pay_ref[2, f, at] = jnp.where(even, last, first)
        other_ref[f, at] = jnp.where(even, first, last)
    for load in loads[1:]:
        load.wait()


def wall_merge_kernel(last, first_round, sent_ref, got_ref, extra_ref, *refs):
    if first_round:
        coef_ref, pay_ref, state_ref = refs
    else:
        old_ref, coef_ref, pay_ref, state_ref = refs
    coef = coef_ref[...]

    def c(j):
        return coef[:, j : j + 1]

    base = 0 if first_round else (16 if last else 8)
    got_r, got_l, halo = got_ref[0], got_ref[1], got_ref[2]
    for j, value in enumerate((c(base) * got_r, c(base + 1) * got_l, c(base + 6) * halo, c(base + 7) * halo)):
        state_ref[j] = value if first_round else old_ref[j] + value
    own_r = c(base + 2) * sent_ref[0] + c(base + 3) * got_r
    own_l = c(base + 4) * sent_ref[1] + c(base + 5) * got_l
    if last:
        pay_ref[0] = c(32) * own_l + c(33) * own_r
        pay_ref[1] = extra_ref[...]
    else:
        pay_ref[0] = own_r
        pay_ref[1] = own_l
        pay_ref[2] = extra_ref[...]


def wall_local_kernel(high_ref, mid_ref, low_ref, table_ref, metric_a, metric_b, out_ref, metric_a_ref, metric_b_ref, sems):
    fields, planes, block, lanes = out_ref.shape
    loads = [pltpu.make_async_copy(metric_a, metric_a_ref, sems.at[0]), pltpu.make_async_copy(metric_b, metric_b_ref, sems.at[1])]
    for load in loads:
        load.start()
    table = table_ref[...].astype(F32)
    lane = lax.broadcasted_iota(jnp.int32, table.shape, 1)
    again = pltpu.roll(table, block, 1)

    def beside(a, b):
        return jnp.concatenate([jnp.where(lane[:block] < block, a[0], b[1]), b[1]], axis=1)[:, : 2 * block].astype(BF16)

    parts = [(table[j * block : (j + 1) * block], again[j * block : (j + 1) * block]) for j in range(3)]
    lhs = jnp.concatenate([beside(parts[0], parts[0]), beside(parts[1], parts[1])], axis=0)
    lhs2 = beside(parts[0], parts[2])

    for f in range(fields):
        high, mid, low = (
            jnp.concatenate([ref[f, q * block : (q + 1) * block] for q in range(planes)], axis=1)
            for ref in (high_ref, mid_ref, low_ref)
        )
        main = dot(lhs, jnp.concatenate([high, mid], axis=0), ((1,), (0,)))
        rest = dot(lhs2, jnp.concatenate([low, high], axis=0), ((1,), (0,)))
        total = main[:block] + (main[block:] + rest)
        for q in range(planes):
            out_ref[f, q] = total[:, q * lanes : (q + 1) * lanes]
    for load in loads:
        load.wait()


def wall_final_kernel(
    local_ref, metric_ref, old_ref, got_ref, coef_ref, table_ref, tail_ref, span_in, out_hbm, span_hbm, buffer, sems
):
    fields, planes, block, lanes = local_ref.shape
    coef = coef_ref[...]
    table = table_ref[...].T[:block]
    enter, leave = (jnp.broadcast_to(table[:, j : j + 1], (block, lanes)) for j in (2, 3))
    top = lax.broadcasted_iota(jnp.int32, (8, lanes), 0) == 0
    bottom = lax.broadcasted_iota(jnp.int32, (8, lanes), 0) == 7

    def c(j):
        return coef[:, j : j + 1]

    copies = [pltpu.make_async_copy(tail_ref, span_hbm.at[fields - 1], sems.at[0])]
    copies[0].start()
    for f in range(fields):
        for start in range(0, planes, STEP):
            at = slice(start, start + STEP)
            got, halo = got_ref[0, f, at], got_ref[1, f, at]
            m, n = old_ref[0, f, at] + c(24) * got, old_ref[1, f, at] + c(25) * got
            first, last = old_ref[2, f, at] + c(30) * halo, old_ref[3, f, at] + c(31) * halo
            for j in range(STEP):
                q, row = start + j, slice(j, j + 1)
                for lo, hi in ((0, 8), (8, block - 8), (block - 8, block)):
                    total = local_ref[f, q, lo:hi] + (enter[lo:hi] * m[row] + leave[lo:hi] * n[row])
                    if lo == 0:
                        total = total + jnp.where(top, first[row], 0.0)
                    if hi == block:
                        total = total + jnp.where(bottom, last[row], 0.0)
                    buffer[f, q, lo:hi] = metric_ref[q, lo:hi] * total
            copies.append(pltpu.make_async_copy(buffer.at[f, at], out_hbm.at[f, at], sems.at[len(copies)]))
            copies[-1].start()
    for copy in copies:
        copy.wait()


def span_moment_kernel(x_ref, table_ref, pay_ref, other_ref, high_ref, mid_ref, low_ref):
    fields, planes, rows, columns = x_ref.shape
    even = lax.axis_index("span") % 2 == 0
    table = table_ref[...]
    lines = planes * rows
    for f in range(fields):
        flat = x_ref[f].reshape(lines, columns)
        for start in range(0, lines, SPAN_ROWS):
            inside = slice(start, start + SPAN_ROWS)
            high, mid, low = split_parts(flat[inside])
            high_ref[f, inside], mid_ref[f, inside], low_ref[f, inside] = high, mid, low
            main = dot(table, jnp.concatenate([high, mid], axis=1), ((1,), (1,)))
            rest = dot(table[:16, :columns], low, ((1,), (1,)))
            total = main[:8] + (main[8:16] + (main[16:24] + rest[:8]))
            first, last = total[2:3], total[3:4]
            at = slice(f * lines + start, f * lines + start + SPAN_ROWS)
            pay_ref[0:2, at] = total[0:2]
            pay_ref[2:3, at] = jnp.where(even, last, first)
            other_ref[:, at] = jnp.where(even, first, last)


def span_matrices(table):
    n = table.shape[0]
    return (
        jnp.concatenate([table[:, : 2 * n], table[:, : 2 * n]], axis=0),
        jnp.concatenate([table[:, :n], table[:, 2 * n :]], axis=0),
    )


def span_product(weights, high, mid, low):
    n = high.shape[1]
    main = dot(jnp.concatenate([high, mid], axis=1), weights[0], ((1,), (0,)))
    rest = dot(jnp.concatenate([low, high], axis=1), weights[1], ((1,), (0,)))
    return main[:, :n], main[:, n:] + rest


def span_local_kernel(start, high_ref, mid_ref, low_ref, table_ref, out_ref):
    count, planes, rows, n = out_ref.shape
    weights = span_matrices(table_ref[...])
    for j in range(count):
        a, b = span_product(weights, *(ref[start + j] for ref in (high_ref, mid_ref, low_ref)))
        out_ref[j] = (a + b).reshape(planes, rows, n)


def span_merge_kernel(sent_ref, got_ref, other_ref, coef_ref, pay_ref, state_ref):
    coef = coef_ref[...]

    def c(j):
        return coef[:, j : j + 1]

    got_r, got_l, halo = got_ref[0:1], got_ref[1:2], got_ref[2:3]
    for j, value in enumerate((c(0) * got_r, c(1) * got_l, c(6) * halo, c(7) * halo)):
        state_ref[j : j + 1] = value
    own_r = c(2) * sent_ref[0:1] + c(3) * got_r
    own_l = c(4) * sent_ref[1:2] + c(5) * got_l
    pay_ref[0:1] = c(16) * own_l + c(17) * own_r
    pay_ref[1:2] = other_ref[...]


def span_final_kernel(ready, high_ref, mid_ref, low_ref, metric_ref, old_ref, got_ref, coef_ref, table_ref, edge_ref, *refs):
    locals_ref = refs[: len(ready)]
    out_hbm, tail_ref, buffer, sems = refs[len(ready) :]
    planes, rows, n = metric_ref.shape
    fields = high_ref.shape[0]
    coef = coef_ref[...]
    weights = span_matrices(table_ref[...])

    def c(j):
        return coef[:, j : j + 1]

    copies = []
    lines = planes * rows
    own = {f: (ref, j) for ref, group in zip(locals_ref, ready) for j, f in enumerate(group)}
    for f in range(fields):
        line = slice(f * lines, (f + 1) * lines)
        got, halo, old = got_ref[0:1, line], got_ref[1:2, line], old_ref[:, line]
        state = jnp.concatenate(
            [old[0:1] + c(8) * got, old[1:2] + c(9) * got, old[2:3] + c(14) * halo, old[3:4] + c(15) * halo]
            + [jnp.zeros((4, lines), F32)]
        )
        s_high = state.astype(BF16).astype(F32)
        s_rest = state - s_high
        s_mid = s_rest.astype(BF16).astype(F32)
        s_low = s_rest - s_mid
        parts = jnp.concatenate([s_high, s_high, s_mid, s_high, s_mid, s_low], axis=0).astype(BF16)
        edge = dot(parts, edge_ref[...], ((0,), (0,)))
        if f in own:
            ref, j = own[f]
            total = ref[j].reshape(lines, n) + edge
        else:
            a, b = span_product(weights, *(ref[f] for ref in (high_ref, mid_ref, low_ref)))
            total = a + (b + edge)
        total = metric_ref[...] * total.reshape(planes, rows, n)
        if f == fields - 1:
            tail_ref[...] = total
        else:
            buffer[f] = total
            copies.append(pltpu.make_async_copy(buffer.at[f], out_hbm.at[f], sems.at[f]))
            copies[-1].start()
    for copy in copies:
        copy.wait()


def slopes(conserved, wall_metric, span_metric):
    fields, planes, rows, columns = conserved.shape
    wall_pieces, span_pieces = lax.axis_size("wall"), lax.axis_size("span")
    wt = line_tables(rows * wall_pieces, wall_pieces)
    st = line_tables(columns * span_pieces, span_pieces)
    chunks = fields * planes // STEP
    lines = fields * planes * rows
    vmem = pl.BlockSpec(memory_space=pltpu.VMEM)
    hbm = pl.BlockSpec(memory_space=pltpu.HBM)

    def shape(*dims, dtype=F32):
        return jax.ShapeDtypeStruct(dims, dtype)

    def call(kernel, in_specs, out_specs, out_shape, micros, scratch=(), aliases=None):
        return pl.pallas_call(
            kernel,
            in_specs=in_specs,
            out_specs=out_specs,
            out_shape=out_shape,
            scratch_shapes=list(scratch),
            input_output_aliases=aliases or {},
            compiler_params=pltpu.CompilerParams(vmem_limit_bytes=VMEM_LIMIT),
            cost_estimate=pl.CostEstimate(flops=0, transcendentals=0, bytes_accessed=int(micros * 3.0e6)),
        )

    wall_rows = np.zeros((wall_pieces, 8, LANES), np.float32)
    for j, key in enumerate(("right", "left", "enter", "leave")):
        wall_rows[:, j, :rows] = wt[key]
    wall_diag = np.zeros((wall_pieces, 3 * rows, LANES), BF16)
    wall_diag[:, :, :rows] = np.concatenate(split_table(wt["diag"]), axis=1)
    span_diag = np.concatenate(split_table(np.swapaxes(st["diag"], 1, 2)), axis=2)
    pick = np.zeros((span_pieces, 4, columns))
    pick[:, 0], pick[:, 1] = st["right"], st["left"]
    pick[:, 2, 0] = 1.0
    pick[:, 3, columns - 1] = 1.0
    p_high, p_mid, p_low = split_table(pick)
    span_pick = np.zeros((span_pieces, 32, 2 * columns), BF16)
    span_pick[:, 0:4] = np.concatenate([p_high, p_high], axis=2)
    span_pick[:, 8:12] = np.concatenate([p_mid, p_mid], axis=2)
    span_pick[:, 16:20, :columns] = p_low
    spread = np.zeros((span_pieces, 8, columns))
    spread[:, 0], spread[:, 1] = st["enter"], st["leave"]
    spread[:, 2, 0] = 1.0
    spread[:, 3, columns - 1] = 1.0
    e_high, e_mid, e_low = split_table(spread)
    span_edge = np.concatenate([e_high, e_mid, e_high, e_low, e_mid, e_high], axis=1)

    def spread_coefficients(t, pieces):
        c = doubling_coefficients(t, pieces)
        out = np.zeros((pieces, 1, LANES), np.float32)
        out[:, 0, : c.shape[1]] = c
        return out

    def at_hbm(values):
        return [pltpu.with_memory_space_constraint(jnp.asarray(t), pltpu.HBM) for t in values]

    def one(values):
        return [shape(*t.shape[1:], dtype=t.dtype) for t in values]

    tables = [wall_rows, wall_diag, spread_coefficients(wt, wall_pieces)]
    tables = at_hbm(tables + [span_diag, span_pick, span_edge, spread_coefficients(st, span_pieces)])
    grid_values = pltpu.with_memory_space_constraint(conserved, pltpu.HBM)

    state = shape(4, fields, planes, columns)
    moment = shape(3, fields, planes, columns)
    out = call(
        wall_moment_kernel,
        [hbm] * 8,
        [vmem] * 10,
        one(tables) + [shape(*conserved.shape), moment, shape(fields, planes, columns)],
        2.5,
        [pltpu.SemaphoreType.DMA((chunks,)), pltpu.SemaphoreType.DMA((len(tables),))],
    )(grid_values, *tables)
    w_rows, w_diag, w_coef, s_diag, s_pick, s_edge, s_coef, x, pay_w, other_w = out

    def swap(flip, pieces):
        return [(k, k ^ flip) for k in range(pieces)]

    got_w = lax.ppermute(pay_w, "wall", swap(1, wall_pieces))

    part = shape(fields, planes * rows, columns, dtype=BF16)
    pay_s, other_s, *parts = call(
        span_moment_kernel, [vmem] * 2, [vmem] * 5, [shape(3, lines), shape(1, lines)] + [part] * 3, 2.0
    )(x, s_pick)
    got_s = lax.ppermute(pay_s, "span", swap(1, span_pieces))

    pay_w, state_w = call(
        functools.partial(wall_merge_kernel, False, True), [vmem] * 4, [vmem] * 2, [moment, state], 0.2
    )(pay_w, got_w, other_w, w_coef)
    got_w = lax.ppermute(pay_w, "wall", swap(3, wall_pieces))
    halo = got_w[2]

    local_w, span_metric, wall_metric = call(
        wall_local_kernel, [vmem] * 4 + [hbm] * 2, [vmem] * 3,
        [shape(*conserved.shape)] + [shape(*wall_metric.shape)] * 2, 1.7,
        [pltpu.SemaphoreType.DMA((2,))],
    )(*parts, w_diag, *(pltpu.with_memory_space_constraint(m, pltpu.HBM) for m in (span_metric, wall_metric)))

    def span_local(group):
        return call(
            functools.partial(span_local_kernel, group[0]), [vmem] * 4, vmem,
            shape(len(group), planes, rows, columns), 0.6 * len(group),
        )(*parts, s_diag)

    own_s = [span_local(group) for group in READY]

    pay_s, state_s = call(
        span_merge_kernel, [vmem] * 4, [vmem] * 2, [shape(2, lines), shape(4, lines)], 0.2
    )(pay_s, got_s, other_s, s_coef)
    got_s = lax.ppermute(pay_s, "span", swap(3, span_pieces))

    pay_w, state_w = call(
        functools.partial(wall_merge_kernel, False, False), [vmem] * 5, [vmem] * 2, [moment, state], 0.2
    )(pay_w, got_w, halo, state_w, w_coef)
    got_w = lax.ppermute(pay_w, "wall", swap(4, wall_pieces))

    pay_w, state_w = call(
        functools.partial(wall_merge_kernel, True, False), [vmem] * 5, [vmem] * 2,
        [shape(2, fields, planes, columns), state], 0.2,
    )(pay_w, got_w, halo, state_w, w_coef)
    got_w = lax.ppermute(pay_w, "wall", swap(12, wall_pieces))

    span_slope, tail = call(
        functools.partial(span_final_kernel, READY), [vmem] * (9 + len(READY)), [hbm, vmem],
        [shape(*conserved.shape), shape(planes, rows, columns)], 3.0,
        [pltpu.VMEM((fields - 1, planes, rows, columns), F32), pltpu.SemaphoreType.DMA((fields,))],
    )(*parts, span_metric, state_s, got_s, s_coef, s_diag, s_edge, *own_s)
    wall_slope, span_slope = call(
        wall_final_kernel, [vmem] * 7 + [hbm], [hbm] * 2, [shape(*conserved.shape)] * 2, 2.4,
        [pltpu.VMEM(conserved.shape, F32), pltpu.SemaphoreType.DMA((chunks + 1,))], {7: 1},
    )(local_w, wall_metric, state_w, got_w, w_coef, w_rows, tail, span_slope)
    return (wall_slope, span_slope)


def solution(mesh):
    in_specs = (
        P(None, "stream", "wall", "span"),
        P("stream", "wall", "span"),
        P("stream", "wall", "span"),
    )
    out_specs = (P(None, "stream", "wall", "span"), P(None, "stream", "wall", "span"))
    return jax.shard_map(slopes, mesh=mesh, in_specs=in_specs, out_specs=out_specs, check_vma=False)
```
